128 devices in a mesh: region: 8 (over y, core), local: 16 (over z, x).
Axes of the slice: x: 4, y: 4, z: 4, core: 2. Of those that a mesh axis runs over, the one named last changes fastest.
Arguments:
- block_flags: int32 [32, 768], P(None, ('region', 'local')), may hold values 0 or 1
- trace: bfloat16 [32, 98304], P(None, ('region', 'local')), may hold values from 0.099609375 to 1
- w_region: bfloat16 [8, 12288, 12288], P('region', None, 'local'), may hold values from -0.0546875 to 0.0546875
- lr_weight: bfloat16 [8, 16, 8, 8, 128, 128], P('region', 'local'), may hold values from -0.1875 to 0.1875
- lr_source: int32 [8, 16, 8, 8], P('region', 'local'), may hold values from 0 to 5
- lr_target: int32 [8, 16, 8, 8], P('region', 'local'), may hold values from 0 to 95
- lr_count: int32 [8, 16, 8], P('region', 'local'), may hold values from 0 to 8, as said below
- g_decay: float32 [98304], P(('region', 'local')), may hold values from 0.5 to 0.97
- v_decay: float32 [98304], P(('region', 'local')), may hold values from 0.4 to 0.95
- g_start: float32 [98304], P(('region', 'local')), may hold values from -6 to 6
- v_start: float32 [98304], P(('region', 'local')), may hold values from -6 to 6
Outputs:
- membrane: float32 [32, 98304], P(None, ('region', 'local'))
- g_final: float32 [98304], P(('region', 'local'))
The draws below stay inside these ranges and needn't reach their ends.
Inputs may be any that keep to these rules, and one draw needn't show every extreme that they name: lr_count is 0 for a region's own devices, exactly 8 from every device to the next region (d = (r + 1) % 8), and 1 to 8 otherwise.
All inputs are finite; a program needn't handle non-finite values. No bound on the sum of `block_flags` on one device may be relied on, other than what follows from the above.
Results may differ from the reference program's by a relative error of at most 0.0003.
Values may be sent and summed in bfloat16 or wider, within the bound.
A program may use at most 128 MiB of HBM per device.

```python
import math
import jax
import jax.numpy as jnp
from jax import lax

B = 128
NB_DEV = 6
STEPS = 32
CAP = 8
REGIONS = 8
LOCALS = 16
BLOCKS_REGION = 96
ALLBLOCKS = 768
NEURONS = 98304


def draw_lr_count(key, part):
    shape = (REGIONS, LOCALS, REGIONS)
    source_region = jax.lax.broadcasted_iota(jnp.int32, shape, 0)
    dest_region = jax.lax.broadcasted_iota(jnp.int32, shape, 2)
    counts = jax.random.randint(jax.random.fold_in(key, 17), shape, 1, CAP + 1).astype(jnp.int32)
    counts = jnp.where(dest_region == (source_region + 1) % REGIONS, CAP, counts)
    counts = jnp.where(dest_region == source_region, 0, counts)
    return counts.astype(jnp.int32)


def place_ends(array, own_key, smallest, largest):
    place = [jax.random.randint(jax.random.fold_in(own_key, axis), (), 0, length) for axis, length in enumerate(array.shape)]
    main_axis = array.shape.index(max(array.shape))
    neighbour = place[:main_axis] + [(place[main_axis] + 1) % array.shape[main_axis]] + place[main_axis + 1:]
    return array.at[tuple(place)].set(smallest).at[tuple(neighbour)].set(largest)


def block_levels(rng, extent, cuts, smallest, top_value):
    loudness, own = 1.0, jax.random.fold_in(rng, 6)
    for dim, shards_of in cuts:
        draws = jnp.exp(jax.random.uniform(jax.random.fold_in(own, dim), (shards_of,), jnp.float32, smallest / len(cuts), top_value / len(cuts)))
        loudness = loudness * jnp.repeat(draws, extent[dim] // shards_of).reshape([-1 if axis == dim else 1 for axis in range(len(extent))])
    return loudness


def noise(key, shape, width, most, pieces=(), held_as=jnp.bfloat16):
    gain = block_levels(key, shape, pieces, -0.22, 0.18) if pieces else 1.0
    values = jax.random.normal(key, shape, jnp.float32) * width * gain
    return jnp.minimum(jnp.maximum(values, -most), most).astype(held_as)


def setup_inputs(seed: int = 0) -> dict:
    key_of = jax.random.split(jax.random.key(seed), 12)
    block_flags = place_ends((jax.random.randint(key_of[0], (STEPS, ALLBLOCKS), 0, 2) < 1).astype(jnp.int32), jax.random.fold_in(key_of[0], 1), 0, 1)
    trace = jnp.clip(jnp.exp(math.log(1.0) - 2.306499 * jax.random.uniform(key_of[1], (STEPS, NEURONS), jnp.float32) ** block_levels(key_of[1], (STEPS, NEURONS), ((1, 128),), -0.2, 0.2)), 0.099609375, 1.0).astype(jnp.bfloat16)
    w_region = noise(key_of[2], (REGIONS, BLOCKS_REGION * B, BLOCKS_REGION * B), (BLOCKS_REGION * B) ** -0.5, 0.0546875, ((0, 8), (2, 16)))
    lr_weight = noise(key_of[3], (REGIONS, LOCALS, REGIONS, CAP, B, B), (B * CAP) ** -0.5, 0.1875, ((0, 8), (1, 16)))
    lr_source = place_ends(jax.random.randint(key_of[4], (REGIONS, LOCALS, REGIONS, CAP), 0, NB_DEV), jax.random.fold_in(key_of[4], 1), 0, NB_DEV - 1).astype(jnp.int32)
    lr_target = place_ends(jax.random.randint(key_of[5], (REGIONS, LOCALS, REGIONS, CAP), 0, BLOCKS_REGION), jax.random.fold_in(key_of[5], 1), 0, BLOCKS_REGION - 1).astype(jnp.int32)
    lr_count = draw_lr_count(jax.random.fold_in(key_of[11], 71), 0)
    g_decay = jnp.clip(jnp.exp(math.log(0.97) - 0.662688 * jax.random.uniform(key_of[7], (NEURONS,), jnp.float32) ** block_levels(key_of[7], (NEURONS,), ((0, 128),), -0.2, 0.2)), 0.5, 0.97)
    v_decay = jnp.clip(jnp.exp(math.log(0.95) - 0.8649974 * jax.random.uniform(key_of[8], (NEURONS,), jnp.float32) ** block_levels(key_of[8], (NEURONS,), ((0, 128),), -0.2, 0.2)), 0.4, 0.95)
    g_start = noise(key_of[9], (NEURONS,), 1.0, 6.0, ((0, 128),), jnp.float32)
    v_start = noise(key_of[10], (NEURONS,), 1.0, 6.0, ((0, 128),), jnp.float32)
    return dict(block_flags=block_flags, trace=trace, w_region=w_region, lr_weight=lr_weight, lr_source=lr_source, lr_target=lr_target, lr_count=lr_count, g_decay=g_decay, v_decay=v_decay, g_start=g_start, v_start=v_start)


def reference(block_flags, trace, w_region, lr_weight, lr_source, lr_target, lr_count, g_decay, v_decay, g_start, v_start):
    flags = jnp.repeat(block_flags, B, axis=1).astype(jnp.bfloat16)
    drive = (flags * trace).astype(jnp.bfloat16)
    by_region = drive.reshape(STEPS, REGIONS, BLOCKS_REGION * B).transpose(1, 0, 2)

    def region_product(pair):
        return jnp.dot(pair[0], pair[1], preferred_element_type=jnp.float32)

    inner = lax.map(region_product, (by_region, w_region))
    inner = inner.transpose(1, 0, 2).reshape(STEPS, NEURONS)

    blocks = drive.reshape(STEPS, REGIONS, LOCALS, NB_DEV, B).transpose(1, 2, 3, 0, 4)
    chosen = jax.vmap(jax.vmap(lambda blk, src: blk[src]))(blocks, lr_source)
    partial_value = jnp.einsum('rldcsi,rldcio->rldcso', chosen.astype(jnp.float32), lr_weight.astype(jnp.float32))
    live = (jnp.arange(CAP, dtype=jnp.int32)[None, None, None, :] < lr_count[:, :, :, None]).astype(jnp.float32)
    partial_value = partial_value * live[:, :, :, :, None, None]
    onehot = (lr_target[..., None] == jnp.arange(BLOCKS_REGION, dtype=jnp.int32)).astype(jnp.float32)
    flat = partial_value.reshape(REGIONS, LOCALS, REGIONS, CAP, STEPS * B)
    outer = jnp.einsum('rldcb,rldcx->dbx', onehot, flat, precision=lax.Precision.HIGHEST)
    outer = outer.reshape(REGIONS, BLOCKS_REGION, STEPS, B).transpose(2, 0, 1, 3).reshape(STEPS, NEURONS)
    current = inner + outer

    def advance(carry, now):
        g_state, v_state = carry
        g_state = g_decay * g_state + (1.0 - g_decay) * now
        v_state = v_decay * v_state + (1.0 - v_decay) * g_state
        return (g_state, v_state), v_state

    (g_last, v_last), membrane = lax.scan(advance, (g_start, v_start), current)
    return membrane, g_last
```

```python
import jax
import jax.numpy as jnp
from jax import lax
from jax.experimental import pallas as pl
from jax.experimental.pallas import tpu as pltpu
from jax.sharding import PartitionSpec as P

MESH = pl.DeviceIdType.MESH
T, B, NB = 32, 128, 6
R, L, Q, CAP = 8, 16, 4, 8
CH = T // Q
ORDER = (4, 3, 5, 2, 6, 1, 7)
LEVELS = 32767.0


def kernel(
    flags, trace, src, cnt, tgt, gd, vd, g0, v0, w_hbm, lrw_hbm,
    out, gfin,
    wv, lrw, dbuf, dblk, idrow, stage, send1, recv1, msend, mrecv,
    send2, recv2, acc, rows,
    wsem, lsem, ag_s, ag_r, d_s, d_r, m_s, m_r, o_s, o_r, own_sem,
):
    r, l = lax.axis_index("region"), lax.axis_index("local")
    z, x = l // Q, l % Q

    barrier = pltpu.get_barrier_semaphore()
    for k in ORDER:
        for i in range(Q):
            pl.semaphore_signal(
                barrier, inc=1, device_id=((r + k) % R, z * Q + i), device_id_type=MESH
            )
    for i in range(1, L):
        pl.semaphore_signal(barrier, inc=1, device_id=(r, (l + i) % L), device_id_type=MESH)

    def lr_copy(n):
        return pltpu.make_async_copy(
            lrw_hbm.at[(r + ORDER[n]) % R], lrw.at[n], lsem.at[n]
        )

    def w_copy(i):
        return pltpu.make_async_copy(
            w_hbm.at[pl.ds(i * (NB * B), NB * B)], wv.at[i], wsem.at[i]
        )

    for n in range(R - 1):
        lr_copy(n).start()
    for dz in range(Q):
        for dx in range(Q):
            w_copy((z + dz) % Q * Q + (x + dx) % Q).start()

    flag_t = flags[...].astype(jnp.float32).T
    for b in range(NB):
        cols = slice(b * B, (b + 1) * B)
        d = (trace[:, cols].astype(jnp.float32) * flag_t[:, b : b + 1]).astype(jnp.bfloat16)
        dblk[b] = d
        dbuf[l, :, cols] = d

    lane = lax.broadcasted_iota(jnp.int32, (R, B), 1)
    idrow[...] = jnp.zeros((R, B), jnp.int32)
    t = tgt[...]
    owner = (t * 43) // 256
    idrow[:, 0:CAP] = owner * 8 + (t - owner * NB) + 1
    ids = pltpu.roll(idrow[...], x * CAP, 1)
    idrow[...] = ids

    pl.semaphore_wait(barrier, (R - 1) * Q + L - 1)

    def ag_copy(block, peer, sem):
        return pltpu.make_async_remote_copy(
            src_ref=dbuf.at[block],
            dst_ref=dbuf.at[block],
            send_sem=ag_s.at[sem],
            recv_sem=ag_r.at[block],
            device_id=(r, peer),
            device_id_type=MESH,
        )

    sent = []

    def go(c):
        c.start()
        sent.append(c)

    for dx in range(1, Q):
        go(ag_copy(l, z * Q + (x + dx) % Q, dx))

    row1 = lax.broadcasted_iota(jnp.int32, (1, B), 1)
    for n, k in enumerate(ORDER):
        d = (r + k) % R
        lr_copy(n).wait()
        st = stage.at[n % 2]
        for j in range(CAP):
            p = jnp.dot(dblk[src[d, j]], lrw[n, j], preferred_element_type=jnp.float32)
            st[pl.ds(j, T, stride=CAP), :] = p
        tiles = st[...].reshape(T, CAP, B)
        peak = jnp.max(jnp.max(jnp.abs(tiles), axis=0), axis=0, keepdims=True)
        factor = LEVELS / jnp.maximum(peak, 1e-30)
        send1[k - 1] = jnp.round(tiles * factor[None]).astype(jnp.int16)
        base = ((k - 1) % Q) * (Q * CAP)
        alive = (row1 - x * CAP) < cnt[0, d]
        row = jnp.where(alive, idrow[pl.ds(d, 1), :], 0)
        msend[k - 1, 0:1, :] = pltpu.roll(row, base, 1).astype(jnp.float32)
        msend[k - 1, 1:2, :] = peak * (1.0 / LEVELS)
        for i in range(Q):
            go(
                pltpu.make_async_remote_copy(
                    src_ref=msend.at[k - 1],
                    dst_ref=mrecv.at[k - 1, x],
                    send_sem=m_s.at[k - 1, i],
                    recv_sem=m_r.at[k - 1, x],
                    device_id=(d, z * Q + i),
                    device_id_type=MESH,
                )
            )
            go(
                pltpu.make_async_remote_copy(
                    src_ref=send1.at[k - 1, pl.ds(i * CH, CH)],
                    dst_ref=recv1.at[k - 1, x],
                    send_sem=d_s.at[k - 1, i],
                    recv_sem=d_r.at[k - 1, x],
                    device_id=(d, z * Q + i),
                    device_id_type=MESH,
                )
            )

    for dx in range(Q):
        block = z * Q + (x + dx) % Q
        if dx:
            ag_copy(block, l, 0).wait_recv()
        for dz in range(1, Q):
            go(ag_copy(block, (z + dz) % Q * Q + x, 4 + dx * 3 + dz - 1))

    acc[...] = jnp.zeros_like(acc)

    def inner(dz, dx, wait):
        i = (z + dz) % Q * Q + (x + dx) % Q
        w_copy(i).wait()
        if wait:
            ag_copy(i, l, 0).wait_recv()
        acc[...] += jnp.dot(dbuf[i], wv[i], preferred_element_type=jnp.float32)

    lax.fori_loop(0, Q, lambda i, c: (inner(0, i, False), c)[1], 0)
    lax.fori_loop(Q, L, lambda i, c: (inner(i // Q, i % Q, True), c)[1], 0)

    for k in range(R - 1):
        for i in range(Q):
            pltpu.make_async_copy(mrecv.at[k, i], mrecv.at[k, i], m_r.at[k, i]).wait()
            pltpu.make_async_copy(recv1.at[k, i], recv1.at[k, i], d_r.at[k, i]).wait()

    place = lax.broadcasted_iota(jnp.int32, (B, B), 0) + 1
    parts = []
    for half, ks in ((0, range(0, 4)), (1, range(4, 7))):
        idv = jnp.zeros((1, B), jnp.float32)
        for k in ks:
            for i in range(Q):
                idv = idv + mrecv[k, i, 0:1, :]
        hot = (place == idv.astype(jnp.int32)).astype(jnp.bfloat16)
        parts.append(hot[:, : len(ks) * Q * CAP])
    hot = jnp.concatenate(parts, axis=1)
    hot2 = jnp.concatenate([hot, hot], axis=1)

    for s in range(0, CH, 2):
        his, los = [], []
        for u in range(2):
            tiles = []
            for k in range(R - 1):
                for i in range(Q):
                    q = recv1[k, i, s + u].astype(jnp.float32)
                    tiles.append(q * mrecv[k, i, 1:2, :])
            f = jnp.concatenate(tiles, axis=0)
            hi = f.astype(jnp.bfloat16)
            his.append(hi)
            los.append((f - hi.astype(jnp.float32)).astype(jnp.bfloat16))
        rhs = jnp.concatenate(
            [jnp.concatenate(his, axis=1), jnp.concatenate(los, axis=1)], axis=0
        )
        res = jnp.dot(hot2, rhs, preferred_element_type=jnp.float32)
        for u in range(2):
            for o in range(L):
                send2[o, s + u] = res[o * 8 : o * 8 + NB, u * B : (u + 1) * B]

    for i in range(1, L):
        o = (l + i) % L
        go(
            pltpu.make_async_remote_copy(
                src_ref=send2.at[o],
                dst_ref=recv2.at[z, pl.ds(x * CH, CH)],
                send_sem=o_s.at[i],
                recv_sem=o_r.at[l],
                device_id=(r, o),
                device_id_type=MESH,
            )
        )
    own = pltpu.make_async_copy(send2.at[l], recv2.at[z, pl.ds(x * CH, CH)], own_sem)
    own.start()

    for b in range(NB):
        rows[pl.ds(b, T, stride=8), :] = acc[:, b * B : (b + 1) * B]

    own.wait()
    for i in range(1, L):
        o = (l + i) % L
        dst = recv2.at[o // Q, pl.ds(o % Q * CH, CH)]
        pltpu.make_async_copy(dst, dst, o_r.at[o]).wait()

    g, v = g0[...], v0[...]
    gdec, vdec = gd[...], vd[...]
    gin, vin = 1.0 - gdec, 1.0 - vdec
    for step in range(T):
        now = rows[step * 8 : step * 8 + NB, :]
        outer = recv2[0, step] + recv2[1, step] + recv2[2, step] + recv2[3, step]
        g = gdec * g + gin * (now + outer)
        v = vdec * v + vin * g
        rows[step * 8 : step * 8 + NB, :] = v
    gfin[...] = g
    for b in range(NB):
        out[:, b * B : (b + 1) * B] = rows[pl.ds(b, T, stride=8), :]

    for c in sent:
        c.wait_send()


def local(
    block_flags, trace, w_region, lr_weight, lr_source, lr_target, lr_count,
    g_decay, v_decay, g_start, v_start,
):
    vmem = pl.BlockSpec(memory_space=pltpu.VMEM)
    smem = pl.BlockSpec(memory_space=pltpu.SMEM)
    hbm = pl.BlockSpec(memory_space=pl.ANY)
    f32, bf16, dma = jnp.float32, jnp.bfloat16, pltpu.SemaphoreType.DMA
    membrane, g_last = pl.pallas_call(
        kernel,
        out_shape=(
            jax.ShapeDtypeStruct((T, NB * B), f32),
            jax.ShapeDtypeStruct((NB, B), f32),
        ),
        in_specs=[vmem, vmem, smem, smem, vmem, vmem, vmem, vmem, vmem, hbm, hbm],
        out_specs=(vmem, vmem),
        scratch_shapes=[
            pltpu.VMEM((L, NB * B, NB * B), bf16),
            pltpu.VMEM((R - 1, CAP, B, B), bf16),
            pltpu.VMEM((L, T, NB * B), bf16),
            pltpu.VMEM((NB, T, B), bf16),
            pltpu.VMEM((R, B), jnp.int32),
            pltpu.VMEM((2, T * CAP, B), f32),
            pltpu.VMEM((R - 1, T, CAP, B), jnp.int16),
            pltpu.VMEM((R - 1, Q, CH, CAP, B), jnp.int16),
            pltpu.VMEM((R - 1, 2, B), f32),
            pltpu.VMEM((R - 1, Q, 2, B), f32),
            pltpu.VMEM((L, CH, NB, B), f32),
            pltpu.VMEM((Q, T, NB, B), f32),
            pltpu.VMEM((T, NB * B), f32),
            pltpu.VMEM((T * 8, B), f32),
            dma((L,)),
            dma((R - 1,)),
            dma((L,)),
            dma((L,)),
            dma((R - 1, Q)),
            dma((R - 1, Q)),
            dma((R - 1, Q)),
            dma((R - 1, Q)),
            dma((L,)),
            dma((L,)),
            dma(()),
        ],
        compiler_params=pltpu.CompilerParams(
            collective_id=0, has_side_effects=True, vmem_limit_bytes=60 * 2**20
        ),
        name="window",
    )(
        block_flags.T,
        trace,
        lr_source.reshape(R, CAP),
        lr_count.reshape(1, R),
        lr_target.reshape(R, CAP),
        g_decay.reshape(NB, B),
        v_decay.reshape(NB, B),
        g_start.reshape(NB, B),
        v_start.reshape(NB, B),
        w_region.reshape(L * NB * B, NB * B),
        lr_weight.reshape(R, CAP, B, B),
    )
    return membrane, g_last.reshape(NB * B)


def solution(mesh):
    return jax.shard_map(
        local,
        mesh=mesh,
        in_specs=(
            P(None, ("region", "local")),
            P(None, ("region", "local")),
            P("region", None, "local"),
            P("region", "local", None, None, None, None),
            P("region", "local", None, None),
            P("region", "local", None, None),
            P("region", "local", None),
            P(("region", "local")),
            P(("region", "local")),
            P(("region", "local")),
            P(("region", "local")),
        ),
        out_specs=(P(None, ("region", "local")), P(("region", "local"))),
        check_vma=False,
    )
```

```python
import jax
import jax.numpy as jnp
from jax import lax
from jax.experimental import pallas as pl
from jax.experimental.pallas import tpu as pltpu
from jax.sharding import PartitionSpec as P

MESH = pl.DeviceIdType.MESH
T, B, NB = 32, 128, 6
R, L, Q, CAP = 8, 16, 4, 8
CH = T // Q
ORDER = (4, 3, 5, 2, 6, 1, 7)
LEVELS = 32767.0
W0, W1, W2 = 4, 8, 8
W_AT = 2
AG_FIRST = True
EARLY = 6
XORDER = (1, 3, 2)
ZORDER = (4, 12, 8, 5, 13, 9, 7, 15, 11, 6, 14, 10)
OUT_ORDER = (10, 6, 14, 9, 11, 2, 8, 5, 7, 13, 15, 1, 3, 4, 12)


def kernel(
    flags_h, trace_h, src_h, cnt_h, tgt_h, gd_h, vd_h, g0_h, v0_h, w_hbm, lrw_hbm,
    out, gfin,
    flags, trace, src, cnt, tgt, gd, vd, g0, v0,
    wv, lrw, dbuf, dblk, idrow, stage, send1, recv1, msend, mrecv,
    stage2, send2, recv2, nsend, nrecv, acc, rows,
    in_sem, wsem, lsem, ag_s, ag_r, d_s, d_r, m_s, m_r, o_s, o_r, n_s, n_r, own_sem,
):
    r, l = lax.axis_index("region"), lax.axis_index("local")
    z, x = l // Q, l % Q

    small = [
        pltpu.make_async_copy(a, b, in_sem.at[n])
        for n, (a, b) in enumerate(
            (
                (trace_h, trace), (flags_h, flags), (src_h, src), (cnt_h, cnt), (tgt_h, tgt),
                (gd_h, gd), (vd_h, vd), (g0_h, g0), (v0_h, v0),
            )
        )
    ]

    def lr_copy(n):
        return pltpu.make_async_copy(
            lrw_hbm.at[(r + ORDER[n]) % R], lrw.at[n], lsem.at[n]
        )

    def member(i):
        return (z + i // Q) % Q * Q + (x + i % Q) % Q

    def w_copy(i):
        m = member(i)
        return pltpu.make_async_copy(
            w_hbm.at[pl.ds(m * (NB * B), NB * B)], wv.at[i], wsem.at[i]
        )

    for c in small[:5]:
        c.start()
    for n in range(R - 1):
        lr_copy(n).start()
    for c in small[5:]:
        c.start()

    barrier = pltpu.get_barrier_semaphore()
    for k in ORDER:
        for i in range(Q):
            pl.semaphore_signal(
                barrier, inc=1, device_id=((r + k) % R, z * Q + i), device_id_type=MESH
            )
    for i in range(1, L):
        pl.semaphore_signal(barrier, inc=1, device_id=(r, (l + i) % L), device_id_type=MESH)

    for i in range(W0):
        w_copy(i).start()

    for c in small[:5]:
        c.wait()
    flag_t = flags[...].astype(jnp.float32).T
    for b in range(NB):
        cols = slice(b * B, (b + 1) * B)
        d = (trace[:, cols].astype(jnp.float32) * flag_t[:, b : b + 1]).astype(jnp.bfloat16)
        dblk[b] = d
        dbuf[l, :, cols] = d

    idrow[...] = jnp.zeros((R, B), jnp.int32)
    t = tgt[...]
    owner = (t * 43) // 256
    idrow[:, 0:CAP] = owner * 8 + (t - owner * NB) + 1
    ids = pltpu.roll(idrow[...], x * CAP, 1)
    idrow[...] = ids

    def ag_copy(block, peer, sem):
        return pltpu.make_async_remote_copy(
            src_ref=dbuf.at[block],
            dst_ref=dbuf.at[block],
            send_sem=ag_s.at[sem],
            recv_sem=ag_r.at[block],
            device_id=(r, peer),
            device_id_type=MESH,
        )

    sent = []

    def go(c):
        c.start()
        sent.append(c)

    def own_drive():
        for dx in (2, 1, 3):
            go(ag_copy(l, z * Q + (x + dx) % Q, dx))
        for dz in (2, 1, 3):
            go(ag_copy(l, (z + dz) % Q * Q + x, 3 + dz))

    def tiles_out(k):
        d = (r + k) % R
        for i in range(Q):
            go(
                pltpu.make_async_remote_copy(
                    src_ref=msend.at[k - 1],
                    dst_ref=mrecv.at[k - 1, x],
                    send_sem=m_s.at[k - 1, i],
                    recv_sem=m_r.at[k - 1, x],
                    device_id=(d, z * Q + i),
                    device_id_type=MESH,
                )
            )
            go(
                pltpu.make_async_remote_copy(
                    src_ref=send1.at[k - 1, pl.ds(i * CH, CH)],
                    dst_ref=recv1.at[k - 1, x],
                    send_sem=d_s.at[k - 1, i],
                    recv_sem=d_r.at[k - 1, x],
                    device_id=(d, z * Q + i),
                    device_id_type=MESH,
                )
            )

    row1 = lax.broadcasted_iota(jnp.int32, (1, B), 1)
    for n, k in enumerate(ORDER):
        d = (r + k) % R
        lr_copy(n).wait()
        st = stage.at[n % 2]
        for j in range(CAP):
            p = jnp.dot(dblk[src[d, j]], lrw[n, j], preferred_element_type=jnp.float32)
            st[pl.ds(j, T, stride=CAP), :] = p
        tiles = st[...].reshape(T, CAP, B)
        peak = jnp.max(jnp.max(jnp.abs(tiles), axis=0), axis=0, keepdims=True)
        factor = LEVELS / jnp.maximum(peak, 1e-30)
        send1[k - 1] = jnp.round(tiles * factor[None]).astype(jnp.int16)
        base = ((k - 1) % Q) * (Q * CAP)
        alive = (row1 - x * CAP) < cnt[0, d]
        row = jnp.where(alive, idrow[pl.ds(d, 1), :], 0)
        msend[k - 1, 0:1, :] = pltpu.roll(row, base, 1).astype(jnp.float32)
        msend[k - 1, 1:2, :] = peak * (1.0 / LEVELS)
        if n == W_AT:
            pl.semaphore_wait(barrier, (R - 1) * Q + L - 1)
            if AG_FIRST:
                own_drive()
            for kk in ORDER[: n + 1]:
                tiles_out(kk)
        if n > W_AT:
            tiles_out(k)
    if not AG_FIRST:
        own_drive()

    for i in range(W0, W1):
        w_copy(i).start()
    acc[...] = jnp.zeros_like(acc)

    def inner(i):
        w_copy(i).wait()
        if W2 and i + W2 < L and i + W2 >= W1:
            w_copy(i + W2).start()
        acc[...] += jnp.dot(dbuf[member(i)], wv[i], preferred_element_type=jnp.float32)

    inner(0)
    for dx in XORDER:
        block = member(dx)
        ag_copy(block, l, 0).wait_recv()
        for dz in (2, 1, 3):
            go(ag_copy(block, (z + dz) % Q * Q + x, 4 + dx * 3 + dz - 1))
        inner(dx)

    def from_z(i):
        ag_copy(member(i), l, 0).wait_recv()
        inner(i)

    for i in ZORDER[:EARLY]:
        from_z(i)

    for k in range(R - 1):
        for i in range(Q):
            pltpu.make_async_copy(mrecv.at[k, i], mrecv.at[k, i], m_r.at[k, i]).wait()
            pltpu.make_async_copy(recv1.at[k, i], recv1.at[k, i], d_r.at[k, i]).wait()

    place = lax.broadcasted_iota(jnp.int32, (B, B), 0) + 1
    parts = []
    for ks in (range(0, 4), range(4, 7)):
        idv = jnp.zeros((1, B), jnp.float32)
        for k in ks:
            for i in range(Q):
                idv = idv + mrecv[k, i, 0:1, :]
        hot = (place == idv.astype(jnp.int32)).astype(jnp.bfloat16)
        parts.append(hot[:, : len(ks) * Q * CAP])
    hot = jnp.concatenate(parts, axis=1)
    hot2 = jnp.concatenate([hot, hot], axis=1)

    for s in range(0, CH, 2):
        his, los = [], []
        for u in range(2):
            tiles = []
            for k in range(R - 1):
                for i in range(Q):
                    q = recv1[k, i, s + u].astype(jnp.float32)
                    tiles.append(q * mrecv[k, i, 1:2, :])
            f = jnp.concatenate(tiles, axis=0)
            hi = f.astype(jnp.bfloat16)
            his.append(hi)
            los.append((f - hi.astype(jnp.float32)).astype(jnp.bfloat16))
        rhs = jnp.concatenate(
            [jnp.concatenate(his, axis=1), jnp.concatenate(los, axis=1)], axis=0
        )
        res = jnp.dot(hot2, rhs, preferred_element_type=jnp.float32)
        for u in range(2):
            for o in range(L):
                stage2[pl.ds(o * 64 + s + u, 8, stride=8), :] = res[
                    o * 8 : o * 8 + 8, u * B : (u + 1) * B
                ]
    for o in range(L):
        f = stage2[o * 64 : o * 64 + NB * CH, :]
        peak = jnp.max(jnp.abs(f), axis=0, keepdims=True)
        send2[o] = jnp.round(f * (LEVELS / jnp.maximum(peak, 1e-30))).astype(jnp.int16)
        nsend[o] = peak * (1.0 / LEVELS)

    for i in OUT_ORDER:
        o = member(i)
        go(
            pltpu.make_async_remote_copy(
                src_ref=nsend.at[o],
                dst_ref=nrecv.at[l],
                send_sem=n_s.at[i],
                recv_sem=n_r.at[l],
                device_id=(r, o),
                device_id_type=MESH,
            )
        )
        go(
            pltpu.make_async_remote_copy(
                src_ref=send2.at[o],
                dst_ref=recv2.at[l],
                send_sem=o_s.at[i],
                recv_sem=o_r.at[l],
                device_id=(r, o),
                device_id_type=MESH,
            )
        )
    own = [
        pltpu.make_async_copy(send2.at[l], recv2.at[l], own_sem.at[0]),
        pltpu.make_async_copy(nsend.at[l], nrecv.at[l], own_sem.at[1]),
    ]
    for c in own:
        c.start()

    for i in ZORDER[EARLY:]:
        from_z(i)

    for c in small[5:]:
        c.wait()
    for c in own:
        c.wait()
    for i in OUT_ORDER:
        o = member(i)
        pltpu.make_async_copy(nrecv.at[o], nrecv.at[o], n_r.at[o]).wait()
        pltpu.make_async_copy(recv2.at[o], recv2.at[o], o_r.at[o]).wait()

    for c in range(Q):
        f = jnp.zeros((NB * CH, B), jnp.float32)
        for zz in range(Q):
            f = f + recv2[zz * Q + c].astype(jnp.float32) * nrecv[zz * Q + c]
        for b in range(NB):
            rows[pl.ds(c * CH * 8 + b, CH, stride=8), :] = (
                acc[c * CH : (c + 1) * CH, b * B : (b + 1) * B] + f[b * CH : (b + 1) * CH]
            )

    g, v = g0[...], v0[...]
    gdec, vdec = gd[...], vd[...]
    gin, vin = 1.0 - gdec, 1.0 - vdec
    for step in range(T):
        g = gdec * g + gin * rows[step * 8 : step * 8 + NB, :]
        v = vdec * v + vin * g
        rows[step * 8 : step * 8 + NB, :] = v
    gfin[...] = g
    for b in range(NB):
        out[:, b * B : (b + 1) * B] = rows[pl.ds(b, T, stride=8), :]

    for c in sent:
        c.wait_send()


def local(
    block_flags, trace, w_region, lr_weight, lr_source, lr_target, lr_count,
    g_decay, v_decay, g_start, v_start,
):
    vmem = pl.BlockSpec(memory_space=pltpu.VMEM)
    hbm = pl.BlockSpec(memory_space=pltpu.HBM)
    f32, bf16, i16, i32 = jnp.float32, jnp.bfloat16, jnp.int16, jnp.int32
    dma = pltpu.SemaphoreType.DMA
    membrane, g_last = pl.pallas_call(
        kernel,
        out_shape=(
            jax.ShapeDtypeStruct((T, NB * B), f32),
            jax.ShapeDtypeStruct((NB, B), f32),
        ),
        in_specs=[hbm] * 11,
        out_specs=(vmem, vmem),
        scratch_shapes=[
            pltpu.VMEM((NB, T), i32),
            pltpu.VMEM((T, NB * B), bf16),
            pltpu.SMEM((R, CAP), i32),
            pltpu.SMEM((1, R), i32),
            pltpu.VMEM((R, CAP), i32),
            pltpu.VMEM((NB, B), f32),
            pltpu.VMEM((NB, B), f32),
            pltpu.VMEM((NB, B), f32),
            pltpu.VMEM((NB, B), f32),
            pltpu.VMEM((L, NB * B, NB * B), bf16),
            pltpu.VMEM((R - 1, CAP, B, B), bf16),
            pltpu.VMEM((L, T, NB * B), bf16),
            pltpu.VMEM((NB, T, B), bf16),
            pltpu.VMEM((R, B), i32),
            pltpu.VMEM((2, T * CAP, B), f32),
            pltpu.VMEM((R - 1, T, CAP, B), i16),
            pltpu.VMEM((R - 1, Q, CH, CAP, B), i16),
            pltpu.VMEM((R - 1, 2, B), f32),
            pltpu.VMEM((R - 1, Q, 2, B), f32),
            pltpu.VMEM((L * 64, B), f32),
            pltpu.VMEM((L, NB * CH, B), i16),
            pltpu.VMEM((L, NB * CH, B), i16),
            pltpu.VMEM((L, 1, B), f32),
            pltpu.VMEM((L, 1, B), f32),
            pltpu.VMEM((T, NB * B), f32),
            pltpu.VMEM((T * 8, B), f32),
            dma((9,)),
            dma((L,)),
            dma((R - 1,)),
            dma((L,)),
            dma((L,)),
            dma((R - 1, Q)),
            dma((R - 1, Q)),
            dma((R - 1, Q)),
            dma((R - 1, Q)),
            dma((L,)),
            dma((L,)),
            dma((L,)),
            dma((L,)),
            dma((2,)),
        ],
        compiler_params=pltpu.CompilerParams(
            collective_id=0, has_side_effects=True, vmem_limit_bytes=48 * 2**20
        ),
        name="window",
    )(
        *(
            pltpu.with_memory_space_constraint(a, pltpu.HBM)
            for a in (
                block_flags.T,
                trace,
                lr_source.reshape(R, CAP),
                lr_count.reshape(1, R),
                lr_target.reshape(R, CAP),
                g_decay.reshape(NB, B),
                v_decay.reshape(NB, B),
                g_start.reshape(NB, B),
                v_start.reshape(NB, B),
                w_region.reshape(L * NB * B, NB * B),
                lr_weight.reshape(R, CAP, B, B),
            )
        )
    )
    return membrane, g_last.reshape(NB * B)


def solution(mesh):
    return jax.shard_map(
        local,
        mesh=mesh,
        in_specs=(
            P(None, ("region", "local")),
            P(None, ("region", "local")),
            P("region", None, "local"),
            P("region", "local", None, None, None, None),
            P("region", "local", None, None),
            P("region", "local", None, None),
            P("region", "local", None),
            P(("region", "local")),
            P(("region", "local")),
            P(("region", "local")),
            P(("region", "local")),
        ),
        out_specs=(P(None, ("region", "local")), P(("region", "local"))),
        check_vma=False,
    )
```

```python
import jax
import jax.numpy as jnp
from jax import lax
from jax.experimental import pallas as pl
from jax.experimental.pallas import tpu as pltpu
from jax.sharding import PartitionSpec as P

MESH = pl.DeviceIdType.MESH
T, B, NB = 32, 128, 6
R, L, Q, CAP = 8, 16, 4, 8
CH = T // Q
ORDER = (4, 3, 5, 2, 6, 1, 7)
LEVELS = 32767.0
HALF = NB * B // 2
W0, W1, W2 = 4, 8, 8
W_AT = 2
DIAG = (5, 7, 13, 15, 6, 9, 11, 14, 10)
FIRST = (
    "f01", "f14", "f03", "f1c", "f02", "f18", "c00", "c10", "c01", "c14", "c03", "c1c", "c02",
    "c18",
)
NEXT = (
    "c11", "c04", "c13", "c0c", "c12", "c08",
)
EARLY = 4
W_ORDER = (0, 1, 4, 3, 12, 2, 8) + DIAG
OUT_ORDER = (10, 6, 14, 9, 11, 2, 8, 5, 7, 13, 15, 1, 3, 4, 12)


def kernel(
    flags_h, trace_h, src_h, cnt_h, tgt_h, gd_h, vd_h, g0_h, v0_h, w_hbm, lrw_hbm,
    out, gfin,
    flags, trace, src, cnt, tgt, gd, vd, g0, v0,
    wv, lrw, dbuf, dblk, idrow, stage, send1, recv1, msend, mrecv,
    stage2, send2, recv2, nsend, nrecv, acc, rows,
    in_sem, wsem, lsem, ag_s, ag_r, d_s, d_r, m_s, m_r, o_s, o_r, n_s, n_r, own_sem,
):
    r, l = lax.axis_index("region"), lax.axis_index("local")
    z, x = l // Q, l % Q
    zb, xb = z - z % 2, x - x % 2
    c = z % 2 * 2 + x % 2

    small = [
        pltpu.make_async_copy(a, b, in_sem.at[n])
        for n, (a, b) in enumerate(
            (
                (trace_h, trace), (flags_h, flags), (src_h, src), (cnt_h, cnt), (tgt_h, tgt),
                (gd_h, gd), (vd_h, vd), (g0_h, g0), (v0_h, v0),
            )
        )
    ]

    def lr_copy(n):
        return pltpu.make_async_copy(
            lrw_hbm.at[(r + ORDER[n]) % R], lrw.at[n], lsem.at[n]
        )

    def member(i):
        return (z + i // Q) % Q * Q + (x + i % Q) % Q

    def w_copy(i):
        m = member(i)
        return pltpu.make_async_copy(
            w_hbm.at[pl.ds(m * (NB * B), NB * B)], wv.at[i], wsem.at[i]
        )

    for cp in small[:5]:
        cp.start()
    for n in range(R - 1):
        lr_copy(n).start()
    for cp in small[5:]:
        cp.start()

    barrier = pltpu.get_barrier_semaphore()
    def mate(i):
        return (zb + i // 2) * Q + xb + i % 2

    for k in ORDER:
        for i in range(Q):
            pl.semaphore_signal(
                barrier, inc=1, device_id=((r + k) % R, mate(i)), device_id_type=MESH
            )
    for i in range(1, L):
        pl.semaphore_signal(barrier, inc=1, device_id=(r, (l + i) % L), device_id_type=MESH)

    for i in range(W0):
        w_copy(W_ORDER[i]).start()

    for cp in small[:5]:
        cp.wait()
    flag_t = flags[...].astype(jnp.float32).T
    for b in range(NB):
        cols = slice(b * B, (b + 1) * B)
        d = (trace[:, cols].astype(jnp.float32) * flag_t[:, b : b + 1]).astype(jnp.bfloat16)
        dblk[b] = d
        dbuf[l, b // 3, :, b % 3 * B : (b % 3 + 1) * B] = d

    idrow[...] = jnp.zeros((R, B), jnp.int32)
    t = tgt[...]
    owner = (t * 43) // 256
    idrow[:, 0:CAP] = owner * 8 + (t - owner * NB) + 1
    ids = pltpu.roll(idrow[...], c * CAP, 1)
    idrow[...] = ids

    def ag_copy(h, block, peer):
        return pltpu.make_async_remote_copy(
            src_ref=dbuf.at[block, h],
            dst_ref=dbuf.at[block, h],
            send_sem=ag_s,
            recv_sem=ag_r.at[h, block],
            device_id=(r, peer),
            device_id_type=MESH,
        )

    def remote(src, dst, send, recv, device):
        pltpu.make_async_remote_copy(
            src_ref=src, dst_ref=dst, send_sem=send, recv_sem=recv,
            device_id=device, device_id_type=MESH,
        ).start()

    def drained(ref, sem):
        pltpu.make_async_copy(ref, ref, sem).wait()

    def own_drive():
        for a in (1, 3, 2):
            ag_copy(0, l, member(a)).start()
            ag_copy(1, l, member(Q * a)).start()

    def own_drive2():
        for a in (1, 3, 2):
            ag_copy(0, l, member(Q * a)).start()
            ag_copy(1, l, member(a)).start()

    def tiles_out(k):
        d = (r + k) % R
        for i in range(Q):
            remote(msend.at[k - 1], mrecv.at[k - 1, c], m_s, m_r, (d, mate(i)))
            remote(
                send1.at[k - 1, pl.ds(i * CH, CH)], recv1.at[k - 1, c], d_s, d_r, (d, mate(i))
            )

    row1 = lax.broadcasted_iota(jnp.int32, (1, B), 1)
    for n, k in enumerate(ORDER):
        d = (r + k) % R
        lr_copy(n).wait()
        st = stage.at[n % 2]
        for j in range(CAP):
            p = jnp.dot(dblk[src[d, j]], lrw[n, j], preferred_element_type=jnp.float32)
            st[pl.ds(j, T, stride=CAP), :] = p
        tiles = st[...].reshape(T, CAP, B)
        peak = jnp.max(jnp.max(jnp.abs(tiles), axis=0), axis=0, keepdims=True)
        factor = LEVELS / jnp.maximum(peak, 1e-30)
        send1[k - 1] = jnp.round(tiles * factor[None]).astype(jnp.int16)
        base = ((k - 1) % Q) * (Q * CAP)
        alive = (row1 - c * CAP) < cnt[0, d]
        row = jnp.where(alive, idrow[pl.ds(d, 1), :], 0)
        msend[k - 1, 0:1, :] = pltpu.roll(row, base, 1).astype(jnp.float32)
        msend[k - 1, 1:2, :] = peak * (1.0 / LEVELS)
        if n == W_AT:
            pl.semaphore_wait(barrier, (R - 1) * Q + L - 1)
        if n >= W_AT:
            for m in range(n + 1) if n == W_AT else (n,):
                if m == 0:
                    own_drive()
                tiles_out(ORDER[m])
    own_drive2()

    for i in range(W0, W1):
        w_copy(W_ORDER[i]).start()
    acc[...] = jnp.zeros_like(acc)

    have, loaded = {(0, 0), (1, 0)}, set()

    def arrive(h, i):
        if (h, i) not in have:
            have.add((h, i))
            ag_copy(h, member(i), l).wait_recv()

    def load(i):
        if i not in loaded:
            w_copy(i).wait()
            n = W_ORDER.index(i) + W2
            if W2 and W1 <= n < L:
                w_copy(W_ORDER[n]).start()
            loaded.add(i)

    def do(steps):
        for op in steps:
            h, i = int(op[1]), int(op[2], 16)
            arrive(h, i)
            if op[0] == "f":
                for a in (1, 3, 2):
                    other = (z + a) % Q * Q + x if h == 0 else z * Q + (x + a) % Q
                    ag_copy(h, member(i), other).start()
            else:
                load(i)
                acc[...] += jnp.dot(
                    dbuf[member(i), h],
                    wv[i, pl.ds(h * HALF, HALF)],
                    preferred_element_type=jnp.float32,
                )

    rest = NEXT + tuple(f"c{h}{i:x}" for i in DIAG for h in range(2))
    do(FIRST)
    do(rest[:EARLY])

    drained(mrecv, m_r)
    drained(recv1, d_r)

    place = lax.broadcasted_iota(jnp.int32, (B, B), 0) + 1
    parts = []
    for ks in (range(0, 4), range(4, 7)):
        idv = jnp.zeros((1, B), jnp.float32)
        for k in ks:
            for i in range(Q):
                idv = idv + mrecv[k, i, 0:1, :]
        hot = (place == idv.astype(jnp.int32)).astype(jnp.bfloat16)
        parts.append(hot[:, : len(ks) * Q * CAP])
    hot = jnp.concatenate(parts, axis=1)
    hot2 = jnp.concatenate([hot, hot], axis=1)

    for s in range(0, CH, 2):
        his, los = [], []
        for u in range(2):
            tiles = []
            for k in range(R - 1):
                for i in range(Q):
                    q = recv1[k, i, s + u].astype(jnp.float32)
                    tiles.append(q * mrecv[k, i, 1:2, :])
            f = jnp.concatenate(tiles, axis=0)
            hi = f.astype(jnp.bfloat16)
            his.append(hi)
            los.append((f - hi.astype(jnp.float32)).astype(jnp.bfloat16))
        rhs = jnp.concatenate(
            [jnp.concatenate(his, axis=1), jnp.concatenate(los, axis=1)], axis=0
        )
        res = jnp.dot(hot2, rhs, preferred_element_type=jnp.float32)
        for u in range(2):
            for o in range(L):
                stage2[pl.ds(o * 64 + s + u, 8, stride=8), :] = res[
                    o * 8 : o * 8 + 8, u * B : (u + 1) * B
                ]
    for o in range(L):
        f = stage2[o * 64 : o * 64 + NB * CH, :]
        peak = jnp.max(jnp.abs(f), axis=0, keepdims=True)
        send2[o] = jnp.round(f * (LEVELS / jnp.maximum(peak, 1e-30))).astype(jnp.int16)
        nsend[o] = peak * (1.0 / LEVELS)

    for i in OUT_ORDER:
        o = member(i)
        remote(nsend.at[o], nrecv.at[l], n_s, n_r, (r, o))
        remote(send2.at[o], recv2.at[l], o_s, o_r, (r, o))
    own = [
        pltpu.make_async_copy(send2.at[l], recv2.at[l], own_sem.at[0]),
        pltpu.make_async_copy(nsend.at[l], nrecv.at[l], own_sem.at[1]),
    ]
    for cp in own:
        cp.start()

    do(rest[EARLY:])

    for cp in small[5:]:
        cp.wait()
    for cp in own:
        cp.wait()
    drained(send1, d_s)
    drained(mrecv, m_s)
    drained(dbuf.at[pl.ds(0, L - 1)], ag_s)
    drained(send2.at[pl.ds(0, L - 1)], o_s)
    drained(nsend.at[pl.ds(0, L - 1)], n_s)
    drained(nrecv.at[pl.ds(0, L - 1)], n_r)
    drained(recv2.at[pl.ds(0, L - 1)], o_r)

    for q in range(Q):
        f = jnp.zeros((NB * CH, B), jnp.float32)
        for u in range(Q):
            o = (u // 2 * 2 + q // 2) * Q + u % 2 * 2 + q % 2
            f = f + recv2[o].astype(jnp.float32) * nrecv[o]
        for b in range(NB):
            rows[pl.ds(q * CH * 8 + b, CH, stride=8), :] = (
                acc[q * CH : (q + 1) * CH, b * B : (b + 1) * B] + f[b * CH : (b + 1) * CH]
            )

    g, v = g0[...], v0[...]
    gdec, vdec = gd[...], vd[...]
    gin, vin = 1.0 - gdec, 1.0 - vdec
    for step in range(T):
        g = gdec * g + gin * rows[step * 8 : step * 8 + NB, :]
        v = vdec * v + vin * g
        rows[step * 8 : step * 8 + NB, :] = v
    gfin[...] = g
    for b in range(NB):
        out[:, b * B : (b + 1) * B] = rows[pl.ds(b, T, stride=8), :]


def local(
    block_flags, trace, w_region, lr_weight, lr_source, lr_target, lr_count,
    g_decay, v_decay, g_start, v_start,
):
    vmem = pl.BlockSpec(memory_space=pltpu.VMEM)
    hbm = pl.BlockSpec(memory_space=pltpu.HBM)
    f32, bf16, i16, i32 = jnp.float32, jnp.bfloat16, jnp.int16, jnp.int32
    dma = pltpu.SemaphoreType.DMA
    membrane, g_last = pl.pallas_call(
        kernel,
        out_shape=(
            jax.ShapeDtypeStruct((T, NB * B), f32),
            jax.ShapeDtypeStruct((NB, B), f32),
        ),
        in_specs=[hbm] * 11,
        out_specs=(vmem, vmem),
        scratch_shapes=[
            pltpu.VMEM((NB, T), i32),
            pltpu.VMEM((T, NB * B), bf16),
            pltpu.SMEM((R, CAP), i32),
            pltpu.SMEM((1, R), i32),
            pltpu.VMEM((R, CAP), i32),
            pltpu.VMEM((NB, B), f32),
            pltpu.VMEM((NB, B), f32),
            pltpu.VMEM((NB, B), f32),
            pltpu.VMEM((NB, B), f32),
            pltpu.VMEM((L, NB * B, NB * B), bf16),
            pltpu.VMEM((R - 1, CAP, B, B), bf16),
            pltpu.VMEM((L, 2, T, HALF), bf16),
            pltpu.VMEM((NB, T, B), bf16),
            pltpu.VMEM((R, B), i32),
            pltpu.VMEM((2, T * CAP, B), f32),
            pltpu.VMEM((R - 1, T, CAP, B), i16),
            pltpu.VMEM((R - 1, Q, CH, CAP, B), i16),
            pltpu.VMEM((R - 1, 2, B), f32),
            pltpu.VMEM((R - 1, Q, 2, B), f32),
            pltpu.VMEM((L * 64, B), f32),
            pltpu.VMEM((L, NB * CH, B), i16),
            pltpu.VMEM((L, NB * CH, B), i16),
            pltpu.VMEM((L, 1, B), f32),
            pltpu.VMEM((L, 1, B), f32),
            pltpu.VMEM((T, NB * B), f32),
            pltpu.VMEM((T * 8, B), f32),
            dma((9,)),
            dma((L,)),
            dma((R - 1,)),
            dma(()),
            dma((2, L)),
            dma(()),
            dma(()),
            dma(()),
            dma(()),
            dma(()),
            dma(()),
            dma(()),
            dma(()),
            dma((2,)),
        ],
        compiler_params=pltpu.CompilerParams(
            collective_id=0, has_side_effects=True, vmem_limit_bytes=48 * 2**20
        ),
        name="window",
    )(
        *(
            pltpu.with_memory_space_constraint(a, pltpu.HBM)
            for a in (
                block_flags.T,
                trace,
                lr_source.reshape(R, CAP),
                lr_count.reshape(1, R),
                lr_target.reshape(R, CAP),
                g_decay.reshape(NB, B),
                v_decay.reshape(NB, B),
                g_start.reshape(NB, B),
                v_start.reshape(NB, B),
                w_region.reshape(L * NB * B, NB * B),
                lr_weight.reshape(R, CAP, B, B),
            )
        )
    )
    return membrane, g_last.reshape(NB * B)


def solution(mesh):
    return jax.shard_map(
        local,
        mesh=mesh,
        in_specs=(
            P(None, ("region", "local")),
            P(None, ("region", "local")),
            P("region", None, "local"),
            P("region", "local", None, None, None, None),
            P("region", "local", None, None),
            P("region", "local", None, None),
            P("region", "local", None),
            P(("region", "local")),
            P(("region", "local")),
            P(("region", "local")),
            P(("region", "local")),
        ),
        out_specs=(P(None, ("region", "local")), P(("region", "local"))),
        check_vma=False,
    )
```

```python
import jax
import jax.numpy as jnp
from jax import lax
from jax.experimental import pallas as pl
from jax.experimental.pallas import tpu as pltpu
from jax.sharding import PartitionSpec as P

MESH = pl.DeviceIdType.MESH
T, B, NB = 32, 128, 6
R, L, Q, CAP = 8, 16, 4, 8
CH = T // Q
ORDER = (4, 3, 5, 2, 6, 1, 7)
LEVELS = 32767.0
HALF = NB * B // 2
W0, W1, W2 = 4, 8, 8
W_AT = 1
DIAG = (5, 7, 13, 15, 6, 9, 11, 14, 10)
FIRST = (
    "f01", "f14", "f03", "f1c", "f02", "f18", "c00", "c10", "c01", "c14", "c03", "c1c", "c02",
    "c18",
)
NEXT = (
    "c11", "c04", "c13", "c0c", "c12", "c08",
)
EARLY = 4
W_ORDER = (0, 1, 4, 3, 12, 2, 8) + DIAG
OUT_ORDER = (10, 6, 14, 9, 11, 2, 8, 5, 7, 13, 15, 1, 3, 4, 12)


def kernel(
    flags_h, trace_h, src_h, cnt_h, tgt_h, gd_h, vd_h, g0_h, v0_h, w_hbm, lrw_hbm,
    out, gfin,
    flags, trace, src, cnt, tgt, gd, vd, g0, v0,
    wv, lrw, dbuf, dblk, idrow, stage, send1, recv1, msend, mrecv,
    stage2, send2, recv2, nsend, nrecv, acc, rows,
    in_sem, wsem, lsem, ag_s, ag_r, d_s, d_r, m_s, m_r, o_s, o_r, n_s, n_r, own_sem,
):
    r, l = lax.axis_index("region"), lax.axis_index("local")
    z, x = l // Q, l % Q
    zb, xb = z - z % 2, x - x % 2
    c = z % 2 * 2 + x % 2

    barrier = pltpu.get_barrier_semaphore()
    def mate(i):
        return (zb + i // 2) * Q + xb + i % 2

    for k in ORDER:
        for i in range(Q):
            pl.semaphore_signal(
                barrier, inc=1, device_id=((r + k) % R, mate(i)), device_id_type=MESH
            )
    for i in range(1, L):
        pl.semaphore_signal(barrier, inc=1, device_id=(r, (l + i) % L), device_id_type=MESH)

    small = [
        pltpu.make_async_copy(a, b, in_sem.at[n])
        for n, (a, b) in enumerate(
            (
                (trace_h, trace), (flags_h, flags), (src_h, src), (cnt_h, cnt), (tgt_h, tgt),
                (gd_h, gd), (vd_h, vd), (g0_h, g0), (v0_h, v0),
            )
        )
    ]

    def lr_copy(n):
        return pltpu.make_async_copy(
            lrw_hbm.at[(r + ORDER[n]) % R], lrw.at[n], lsem.at[n]
        )

    def member(i):
        return (z + i // Q) % Q * Q + (x + i % Q) % Q

    def w_copy(i):
        m = member(i)
        return pltpu.make_async_copy(
            w_hbm.at[pl.ds(m * (NB * B), NB * B)], wv.at[i], wsem.at[i]
        )

    for cp in small[:5]:
        cp.start()
    for n in range(R - 1):
        lr_copy(n).start()
    for cp in small[5:]:
        cp.start()

    for i in range(W0):
        w_copy(W_ORDER[i]).start()

    for cp in small[:5]:
        cp.wait()
    flag_t = flags[...].astype(jnp.float32).T
    for b in range(NB):
        cols = slice(b * B, (b + 1) * B)
        d = (trace[:, cols].astype(jnp.float32) * flag_t[:, b : b + 1]).astype(jnp.bfloat16)
        dblk[b] = d
        dbuf[l, b // 3, :, b % 3 * B : (b % 3 + 1) * B] = d

    idrow[...] = jnp.zeros((R, B), jnp.int32)
    t = tgt[...]
    owner = (t * 43) // 256
    idrow[:, 0:CAP] = owner * 8 + (t - owner * NB) + 1
    ids = pltpu.roll(idrow[...], c * CAP, 1)
    idrow[...] = ids

    def ag_copy(h, block, peer):
        return pltpu.make_async_remote_copy(
            src_ref=dbuf.at[block, h],
            dst_ref=dbuf.at[block, h],
            send_sem=ag_s,
            recv_sem=ag_r.at[h, block],
            device_id=(r, peer),
            device_id_type=MESH,
        )

    def remote(src, dst, send, recv, device):
        pltpu.make_async_remote_copy(
            src_ref=src, dst_ref=dst, send_sem=send, recv_sem=recv,
            device_id=device, device_id_type=MESH,
        ).start()

    def drained(ref, sem):
        pltpu.make_async_copy(ref, ref, sem).wait()

    def own_drive():
        for a in (1, 3, 2):
            ag_copy(0, l, member(a)).start()
            ag_copy(1, l, member(Q * a)).start()

    def own_drive2():
        for a in (1, 3, 2):
            ag_copy(0, l, member(Q * a)).start()
            ag_copy(1, l, member(a)).start()

    def tiles_out(k):
        d = (r + k) % R
        for i in range(Q):
            remote(msend.at[k - 1], mrecv.at[k - 1, c], m_s, m_r, (d, mate(i)))
            remote(
                send1.at[k - 1, pl.ds(i * CH, CH)], recv1.at[k - 1, c], d_s, d_r, (d, mate(i))
            )

    row1 = lax.broadcasted_iota(jnp.int32, (1, B), 1)
    for n, k in enumerate(ORDER):
        d = (r + k) % R
        lr_copy(n).wait()
        st = stage.at[n % 2]
        for j in range(CAP):
            p = jnp.dot(dblk[src[d, j]], lrw[n, j], preferred_element_type=jnp.float32)
            st[pl.ds(j, T, stride=CAP), :] = p
        tiles = st[...].reshape(T, CAP, B)
        peak = jnp.max(jnp.max(jnp.abs(tiles), axis=0), axis=0, keepdims=True)
        factor = LEVELS / jnp.maximum(peak, 1e-30)
        send1[k - 1] = jnp.round(tiles * factor[None]).astype(jnp.int16)
        base = ((k - 1) % Q) * (Q * CAP)
        alive = (row1 - c * CAP) < cnt[0, d]
        row = jnp.where(alive, idrow[pl.ds(d, 1), :], 0)
        msend[k - 1, 0:1, :] = pltpu.roll(row, base, 1).astype(jnp.float32)
        msend[k - 1, 1:2, :] = peak * (1.0 / LEVELS)
        if n == W_AT:
            pl.semaphore_wait(barrier, (R - 1) * Q + L - 1)
        if n >= W_AT:
            for m in range(n + 1) if n == W_AT else (n,):
                if m == 0:
                    own_drive()
                tiles_out(ORDER[m])
    own_drive2()

    for i in range(W0, W1):
        w_copy(W_ORDER[i]).start()
    acc[...] = jnp.zeros_like(acc)

    have, loaded = {(0, 0), (1, 0)}, set()

    def arrive(h, i):
        if (h, i) not in have:
            have.add((h, i))
            ag_copy(h, member(i), l).wait_recv()

    def load(i):
        if i not in loaded:
            w_copy(i).wait()
            n = W_ORDER.index(i) + W2
            if W2 and W1 <= n < L:
                w_copy(W_ORDER[n]).start()
            loaded.add(i)

    def do(steps):
        for op in steps:
            h, i = int(op[1]), int(op[2], 16)
            arrive(h, i)
            if op[0] == "f":
                for a in (1, 3, 2):
                    other = (z + a) % Q * Q + x if h == 0 else z * Q + (x + a) % Q
                    ag_copy(h, member(i), other).start()
            else:
                load(i)
                acc[...] += jnp.dot(
                    dbuf[member(i), h],
                    wv[i, pl.ds(h * HALF, HALF)],
                    preferred_element_type=jnp.float32,
                )

    rest = NEXT + tuple(f"c{h}{i:x}" for i in DIAG for h in range(2))
    do(FIRST)
    do(rest[:EARLY])

    drained(mrecv, m_r)
    drained(recv1, d_r)

    place = lax.broadcasted_iota(jnp.int32, (B, B), 0) + 1
    parts = []
    for ks in (range(0, 4), range(4, 7)):
        idv = jnp.zeros((1, B), jnp.float32)
        for k in ks:
            for i in range(Q):
                idv = idv + mrecv[k, i, 0:1, :]
        hot = (place == idv.astype(jnp.int32)).astype(jnp.bfloat16)
        parts.append(hot[:, : len(ks) * Q * CAP])
    hot = jnp.concatenate(parts, axis=1)
    hot2 = jnp.concatenate([hot, hot], axis=1)

    for s in range(0, CH, 2):
        his, los = [], []
        for u in range(2):
            tiles = []
            for k in range(R - 1):
                for i in range(Q):
                    q = recv1[k, i, s + u].astype(jnp.float32)
                    tiles.append(q * mrecv[k, i, 1:2, :])
            f = jnp.concatenate(tiles, axis=0)
            hi = f.astype(jnp.bfloat16)
            his.append(hi)
            los.append((f - hi.astype(jnp.float32)).astype(jnp.bfloat16))
        rhs = jnp.concatenate(
            [jnp.concatenate(his, axis=1), jnp.concatenate(los, axis=1)], axis=0
        )
        res = jnp.dot(hot2, rhs, preferred_element_type=jnp.float32)
        for u in range(2):
            for o in range(L):
                stage2[pl.ds(o * 64 + s + u, 8, stride=8), :] = res[
                    o * 8 : o * 8 + 8, u * B : (u + 1) * B
                ]
    for o in range(L):
        f = stage2[o * 64 : o * 64 + NB * CH, :]
        peak = jnp.max(jnp.abs(f), axis=0, keepdims=True)
        send2[o] = jnp.round(f * (LEVELS / jnp.maximum(peak, 1e-30))).astype(jnp.int16)
        nsend[o] = peak * (1.0 / LEVELS)

    for i in OUT_ORDER:
        o = member(i)
        remote(nsend.at[o], nrecv.at[l], n_s, n_r, (r, o))
        remote(send2.at[o], recv2.at[l], o_s, o_r, (r, o))
    own = [
        pltpu.make_async_copy(send2.at[l], recv2.at[l], own_sem.at[0]),
        pltpu.make_async_copy(nsend.at[l], nrecv.at[l], own_sem.at[1]),
    ]
    for cp in own:
        cp.start()

    do(rest[EARLY:])

    for cp in small[5:]:
        cp.wait()
    for cp in own:
        cp.wait()
    drained(send1, d_s)
    drained(mrecv, m_s)
    drained(dbuf.at[pl.ds(0, L - 1)], ag_s)
    drained(send2.at[pl.ds(0, L - 1)], o_s)
    drained(nsend.at[pl.ds(0, L - 1)], n_s)
    drained(nrecv.at[pl.ds(0, L - 1)], n_r)
    drained(recv2.at[pl.ds(0, L - 1)], o_r)

    for q in range(Q):
        f = jnp.zeros((NB * CH, B), jnp.float32)
        for u in range(Q):
            o = (u // 2 * 2 + q // 2) * Q + u % 2 * 2 + q % 2
            f = f + recv2[o].astype(jnp.float32) * nrecv[o]
        for b in range(NB):
            rows[pl.ds(q * CH * 8 + b, CH, stride=8), :] = (
                acc[q * CH : (q + 1) * CH, b * B : (b + 1) * B] + f[b * CH : (b + 1) * CH]
            )

    g, v = g0[...], v0[...]
    gdec, vdec = gd[...], vd[...]
    gin, vin = 1.0 - gdec, 1.0 - vdec
    for step in range(T):
        g = gdec * g + gin * rows[step * 8 : step * 8 + NB, :]
        v = vdec * v + vin * g
        rows[step * 8 : step * 8 + NB, :] = v
    gfin[...] = g
    for b in range(NB):
        out[:, b * B : (b + 1) * B] = rows[pl.ds(b, T, stride=8), :]


def place(m_ref, g_ref, out, gfin, sem):
    copies = [
        pltpu.make_async_copy(m_ref, out, sem.at[0]),
        pltpu.make_async_copy(g_ref, gfin, sem.at[1]),
    ]
    for cp in copies:
        cp.start()
    for cp in copies:
        cp.wait()


def local(
    block_flags, trace, w_region, lr_weight, lr_source, lr_target, lr_count,
    g_decay, v_decay, g_start, v_start,
):
    vmem = pl.BlockSpec(memory_space=pltpu.VMEM)
    hbm = pl.BlockSpec(memory_space=pltpu.HBM)
    f32, bf16, i16, i32 = jnp.float32, jnp.bfloat16, jnp.int16, jnp.int32
    dma = pltpu.SemaphoreType.DMA
    membrane, g_last = pl.pallas_call(
        kernel,
        out_shape=(
            jax.ShapeDtypeStruct((T, NB * B), f32),
            jax.ShapeDtypeStruct((NB, B), f32),
        ),
        in_specs=[hbm] * 11,
        out_specs=(vmem, vmem),
        scratch_shapes=[
            pltpu.VMEM((NB, T), i32),
            pltpu.VMEM((T, NB * B), bf16),
            pltpu.SMEM((R, CAP), i32),
            pltpu.SMEM((1, R), i32),
            pltpu.VMEM((R, CAP), i32),
            pltpu.VMEM((NB, B), f32),
            pltpu.VMEM((NB, B), f32),
            pltpu.VMEM((NB, B), f32),
            pltpu.VMEM((NB, B), f32),
            pltpu.VMEM((L, NB * B, NB * B), bf16),
            pltpu.VMEM((R - 1, CAP, B, B), bf16),
            pltpu.VMEM((L, 2, T, HALF), bf16),
            pltpu.VMEM((NB, T, B), bf16),
            pltpu.VMEM((R, B), i32),
            pltpu.VMEM((2, T * CAP, B), f32),
            pltpu.VMEM((R - 1, T, CAP, B), i16),
            pltpu.VMEM((R - 1, Q, CH, CAP, B), i16),
            pltpu.VMEM((R - 1, 2, B), f32),
            pltpu.VMEM((R - 1, Q, 2, B), f32),
            pltpu.VMEM((L * 64, B), f32),
            pltpu.VMEM((L, NB * CH, B), i16),
            pltpu.VMEM((L, NB * CH, B), i16),
            pltpu.VMEM((L, 1, B), f32),
            pltpu.VMEM((L, 1, B), f32),
            pltpu.VMEM((T, NB * B), f32),
            pltpu.VMEM((T * 8, B), f32),
            dma((9,)),
            dma((L,)),
            dma((R - 1,)),
            dma(()),
            dma((2, L)),
            dma(()),
            dma(()),
            dma(()),
            dma(()),
            dma(()),
            dma(()),
            dma(()),
            dma(()),
            dma((2,)),
        ],
        compiler_params=pltpu.CompilerParams(
            collective_id=0, has_side_effects=True, vmem_limit_bytes=48 * 2**20
        ),
        name="window",
    )(
        *(
            pltpu.with_memory_space_constraint(a, pltpu.HBM)
            for a in (
                block_flags.T,
                trace,
                lr_source.reshape(R, CAP),
                lr_count.reshape(1, R),
                lr_target.reshape(R, CAP),
                g_decay.reshape(NB, B),
                v_decay.reshape(NB, B),
                g_start.reshape(NB, B),
                v_start.reshape(NB, B),
                w_region.reshape(L * NB * B, NB * B),
                lr_weight.reshape(R, CAP, B, B),
            )
        )
    )
    membrane, g_last = pl.pallas_call(
        place,
        out_shape=(
            jax.ShapeDtypeStruct((T, NB * B), f32),
            jax.ShapeDtypeStruct((NB, B), f32),
        ),
        in_specs=[vmem, vmem],
        out_specs=(hbm, hbm),
        scratch_shapes=[dma((2,))],
        compiler_params=pltpu.CompilerParams(vmem_limit_bytes=2**20),
        name="place",
    )(membrane, g_last)
    return membrane, g_last.reshape(NB * B)


def solution(mesh):
    return jax.shard_map(
        local,
        mesh=mesh,
        in_specs=(
            P(None, ("region", "local")),
            P(None, ("region", "local")),
            P("region", None, "local"),
            P("region", "local", None, None, None, None),
            P("region", "local", None, None),
            P("region", "local", None, None),
            P("region", "local", None),
            P(("region", "local")),
            P(("region", "local")),
            P(("region", "local")),
            P(("region", "local")),
        ),
        out_specs=(P(None, ("region", "local")), P(("region", "local"))),
        check_vma=False,
    )
```

```python
import jax
import jax.numpy as jnp
from jax import lax
from jax.experimental import pallas as pl
from jax.experimental.pallas import tpu as pltpu
from jax.sharding import PartitionSpec as P

MESH = pl.DeviceIdType.MESH
T, B, NB = 32, 128, 6
R, L, Q, CAP = 8, 16, 4, 8
CH = T // Q
ORDER = (4, 3, 5, 2, 6, 1, 7)
LEVELS = 32767.0
HALF = NB * B // 2
W0, W1, W2 = 3, 8, 8
W_AT = 1
DIAG = (5, 7, 13, 15, 6, 9, 11, 14, 10)
FIRST = (
    "f01", "f14", "f03", "f1c", "f02", "f18", "c00", "c10", "c01", "c14", "c03", "c1c", "c02",
    "c18",
)
NEXT = (
    "c11", "c04", "c13", "c0c", "c12", "c08",
)
EARLY = 4
W_ORDER = (0, 1, 4, 3, 12, 2, 8) + DIAG
OUT_ORDER = (10, 6, 14, 9, 11, 2, 8, 5, 7, 13, 15, 1, 3, 4, 12)


def kernel(
    flags_h, trace_h, src_h, cnt_h, tgt_h, gd_h, vd_h, g0_h, v0_h, w_hbm, lrw_hbm,
    out, gfin,
    flags, trace, src, cnt, tgt, gd, vd, g0, v0,
    wv, lrw, dbuf, dblk, idrow, stage, send1, recv1, msend, mrecv,
    stage2, send2, recv2, nsend, nrecv, acc, rows,
    in_sem, wsem, lsem, ag_s, ag_r, d_s, d_r, m_s, m_r, o_s, o_r, n_s, n_r, own_sem,
):
    r, l = lax.axis_index("region"), lax.axis_index("local")
    z, x = l // Q, l % Q
    zb, xb = z - z % 2, x - x % 2
    c = z % 2 * 2 + x % 2

    barrier = pltpu.get_barrier_semaphore()
    def mate(i):
        return (zb + i // 2) * Q + xb + i % 2

    for k in ORDER:
        for i in range(Q):
            pl.semaphore_signal(
                barrier, inc=1, device_id=((r + k) % R, mate(i)), device_id_type=MESH
            )
    for i in range(1, L):
        pl.semaphore_signal(barrier, inc=1, device_id=(r, (l + i) % L), device_id_type=MESH)

    small = [
        pltpu.make_async_copy(a, b, in_sem.at[n])
        for n, (a, b) in enumerate(
            (
                (trace_h, trace), (flags_h, flags), (src_h, src), (cnt_h, cnt), (tgt_h, tgt),
                (gd_h, gd), (vd_h, vd), (g0_h, g0), (v0_h, v0),
            )
        )
    ]

    def lr_copy(n):
        return pltpu.make_async_copy(
            lrw_hbm.at[(r + ORDER[n]) % R], lrw.at[n], lsem.at[n]
        )

    def member(i):
        return (z + i // Q) % Q * Q + (x + i % Q) % Q

    def w_copy(i):
        m = member(i)
        return pltpu.make_async_copy(
            w_hbm.at[pl.ds(m * (NB * B), NB * B)], wv.at[i], wsem.at[i]
        )

    for cp in small[:5]:
        cp.start()
    for n in range(R - 1):
        lr_copy(n).start()
    for cp in small[5:]:
        cp.start()

    for i in range(W0):
        w_copy(W_ORDER[i]).start()

    for cp in small[:5]:
        cp.wait()
    flag_t = flags[...].astype(jnp.float32).T
    for b in range(NB):
        cols = slice(b * B, (b + 1) * B)
        d = (trace[:, cols].astype(jnp.float32) * flag_t[:, b : b + 1]).astype(jnp.bfloat16)
        dblk[b] = d
        dbuf[l, b // 3, :, b % 3 * B : (b % 3 + 1) * B] = d

    idrow[...] = jnp.zeros((R, B), jnp.int32)
    t = tgt[...]
    owner = (t * 43) // 256
    idrow[:, 0:CAP] = owner * 8 + (t - owner * NB) + 1
    ids = pltpu.roll(idrow[...], c * CAP, 1)
    idrow[...] = ids

    def ag_copy(h, block, peer):
        return pltpu.make_async_remote_copy(
            src_ref=dbuf.at[block, h],
            dst_ref=dbuf.at[block, h],
            send_sem=ag_s,
            recv_sem=ag_r.at[h, block],
            device_id=(r, peer),
            device_id_type=MESH,
        )

    def remote(src, dst, send, recv, device):
        pltpu.make_async_remote_copy(
            src_ref=src, dst_ref=dst, send_sem=send, recv_sem=recv,
            device_id=device, device_id_type=MESH,
        ).start()

    def drained(ref, sem):
        pltpu.make_async_copy(ref, ref, sem).wait()

    def own_drive():
        for a in (1, 3, 2):
            ag_copy(0, l, member(a)).start()
            ag_copy(1, l, member(Q * a)).start()

    def own_drive2():
        for a in (1, 3, 2):
            ag_copy(0, l, member(Q * a)).start()
            ag_copy(1, l, member(a)).start()

    def tiles_out(k):
        d = (r + k) % R
        for i in range(Q):
            remote(
                send1.at[k - 1, pl.ds(i * CH, CH)], recv1.at[k - 1, c], d_s, d_r, (d, mate(i))
            )
            remote(msend.at[k - 1], mrecv.at[k - 1, c], m_s, m_r, (d, mate(i)))

    row1 = lax.broadcasted_iota(jnp.int32, (1, B), 1)
    for n, k in enumerate(ORDER):
        d = (r + k) % R
        lr_copy(n).wait()
        st = stage.at[n % 2]
        for j in range(CAP):
            p = jnp.dot(dblk[src[d, j]], lrw[n, j], preferred_element_type=jnp.float32)
            st[pl.ds(j, T, stride=CAP), :] = p
        tiles = st[...].reshape(T, CAP, B)
        peak = jnp.max(jnp.max(jnp.abs(tiles), axis=0), axis=0, keepdims=True)
        factor = LEVELS / jnp.maximum(peak, 1e-30)
        send1[k - 1] = jnp.round(tiles * factor[None]).astype(jnp.int16)
        base = ((k - 1) % Q) * (Q * CAP)
        alive = (row1 - c * CAP) < cnt[0, d]
        row = jnp.where(alive, idrow[pl.ds(d, 1), :], 0)
        msend[k - 1, 0:1, :] = pltpu.roll(row, base, 1).astype(jnp.float32)
        msend[k - 1, 1:2, :] = peak * (1.0 / LEVELS)
        if n == W_AT:
            pl.semaphore_wait(barrier, (R - 1) * Q + L - 1)
        if n >= W_AT:
            for m in range(n + 1) if n == W_AT else (n,):
                if m == 0:
                    own_drive()
                tiles_out(ORDER[m])
    own_drive2()

    for i in range(W0, W1):
        w_copy(W_ORDER[i]).start()
    acc[...] = jnp.zeros_like(acc)

    have, loaded = {(0, 0), (1, 0)}, set()

    def arrive(h, i):
        if (h, i) not in have:
            have.add((h, i))
            ag_copy(h, member(i), l).wait_recv()

    def load(i):
        if i not in loaded:
            w_copy(i).wait()
            n = W_ORDER.index(i) + W2
            if W2 and W1 <= n < L:
                w_copy(W_ORDER[n]).start()
            loaded.add(i)

    def do(steps):
        for op in steps:
            h, i = int(op[1]), int(op[2], 16)
            arrive(h, i)
            if op[0] == "f":
                for a in (1, 3, 2):
                    other = (z + a) % Q * Q + x if h == 0 else z * Q + (x + a) % Q
                    ag_copy(h, member(i), other).start()
            else:
                load(i)
                acc[...] += jnp.dot(
                    dbuf[member(i), h],
                    wv[i, pl.ds(h * HALF, HALF)],
                    preferred_element_type=jnp.float32,
                )

    rest = NEXT + tuple(f"c{h}{i:x}" for i in DIAG for h in range(2))
    do(FIRST)
    do(rest[:EARLY])

    drained(mrecv, m_r)

    place = lax.broadcasted_iota(jnp.int32, (B, B), 0) + 1
    parts = []
    for ks in (range(0, 4), range(4, 7)):
        idv = jnp.zeros((1, B), jnp.float32)
        for k in ks:
            for i in range(Q):
                idv = idv + mrecv[k, i, 0:1, :]
        hot = (place == idv.astype(jnp.int32)).astype(jnp.bfloat16)
        parts.append(hot[:, : len(ks) * Q * CAP])
    hot = jnp.concatenate(parts, axis=1)
    hot2 = jnp.concatenate([hot, hot], axis=1)

    drained(recv1, d_r)
    for s in range(0, CH, 2):
        his, los = [], []
        for u in range(2):
            tiles = []
            for k in range(R - 1):
                for i in range(Q):
                    q = recv1[k, i, s + u].astype(jnp.float32)
                    tiles.append(q * mrecv[k, i, 1:2, :])
            f = jnp.concatenate(tiles, axis=0)
            hi = f.astype(jnp.bfloat16)
            his.append(hi)
            los.append((f - hi.astype(jnp.float32)).astype(jnp.bfloat16))
        rhs = jnp.concatenate(
            [jnp.concatenate(his, axis=1), jnp.concatenate(los, axis=1)], axis=0
        )
        res = jnp.dot(hot2, rhs, preferred_element_type=jnp.float32)
        for u in range(2):
            for o in range(L):
                stage2[pl.ds(o * 64 + s + u, 8, stride=8), :] = res[
                    o * 8 : o * 8 + 8, u * B : (u + 1) * B
                ]
    for o in range(L):
        f = stage2[o * 64 : o * 64 + NB * CH, :]
        peak = jnp.max(jnp.abs(f), axis=0, keepdims=True)
        send2[o] = jnp.round(f * (LEVELS / jnp.maximum(peak, 1e-30))).astype(jnp.int16)
        nsend[o] = peak * (1.0 / LEVELS)

    for i in OUT_ORDER:
        o = member(i)
        remote(send2.at[o], recv2.at[l], o_s, o_r, (r, o))
        remote(nsend.at[o], nrecv.at[l], n_s, n_r, (r, o))
    own = [
        pltpu.make_async_copy(send2.at[l], recv2.at[l], own_sem.at[0]),
        pltpu.make_async_copy(nsend.at[l], nrecv.at[l], own_sem.at[1]),
    ]
    for cp in own:
        cp.start()

    do(rest[EARLY:])

    for cp in small[5:]:
        cp.wait()
    for cp in own:
        cp.wait()
    drained(send1, d_s)
    drained(mrecv, m_s)
    drained(dbuf.at[pl.ds(0, L - 1)], ag_s)
    drained(send2.at[pl.ds(0, L - 1)], o_s)
    drained(nsend.at[pl.ds(0, L - 1)], n_s)
    drained(nrecv.at[pl.ds(0, L - 1)], n_r)
    drained(recv2.at[pl.ds(0, L - 1)], o_r)

    for q in range(Q):
        f = jnp.zeros((NB * CH, B), jnp.float32)
        for u in range(Q):
            o = (u // 2 * 2 + q // 2) * Q + u % 2 * 2 + q % 2
            f = f + recv2[o].astype(jnp.float32) * nrecv[o]
        for b in range(NB):
            rows[pl.ds(q * CH * 8 + b, CH, stride=8), :] = (
                acc[q * CH : (q + 1) * CH, b * B : (b + 1) * B] + f[b * CH : (b + 1) * CH]
            )

    g, v = g0[...], v0[...]
    gdec, vdec = gd[...], vd[...]
    gin, vin = 1.0 - gdec, 1.0 - vdec
    for step in range(T):
        g = gdec * g + gin * rows[step * 8 : step * 8 + NB, :]
        v = vdec * v + vin * g
        rows[step * 8 : step * 8 + NB, :] = v
    gfin[...] = g
    for b in range(NB):
        out[:, b * B : (b + 1) * B] = rows[pl.ds(b, T, stride=8), :]


def place(m_ref, g_ref, out, gfin, sem):
    copies = [
        pltpu.make_async_copy(m_ref, out, sem.at[0]),
        pltpu.make_async_copy(g_ref, gfin, sem.at[1]),
    ]
    for cp in copies:
        cp.start()
    for cp in copies:
        cp.wait()


def local(
    block_flags, trace, w_region, lr_weight, lr_source, lr_target, lr_count,
    g_decay, v_decay, g_start, v_start,
):
    vmem = pl.BlockSpec(memory_space=pltpu.VMEM)
    hbm = pl.BlockSpec(memory_space=pltpu.HBM)
    f32, bf16, i16, i32 = jnp.float32, jnp.bfloat16, jnp.int16, jnp.int32
    dma = pltpu.SemaphoreType.DMA
    membrane, g_last = pl.pallas_call(
        kernel,
        out_shape=(
            jax.ShapeDtypeStruct((T, NB * B), f32),
            jax.ShapeDtypeStruct((NB, B), f32),
        ),
        in_specs=[hbm] * 11,
        out_specs=(vmem, vmem),
        scratch_shapes=[
            pltpu.VMEM((NB, T), i32),
            pltpu.VMEM((T, NB * B), bf16),
            pltpu.SMEM((R, CAP), i32),
            pltpu.SMEM((1, R), i32),
            pltpu.VMEM((R, CAP), i32),
            pltpu.VMEM((NB, B), f32),
            pltpu.VMEM((NB, B), f32),
            pltpu.VMEM((NB, B), f32),
            pltpu.VMEM((NB, B), f32),
            pltpu.VMEM((L, NB * B, NB * B), bf16),
            pltpu.VMEM((R - 1, CAP, B, B), bf16),
            pltpu.VMEM((L, 2, T, HALF), bf16),
            pltpu.VMEM((NB, T, B), bf16),
            pltpu.VMEM((R, B), i32),
            pltpu.VMEM((2, T * CAP, B), f32),
            pltpu.VMEM((R - 1, T, CAP, B), i16),
            pltpu.VMEM((R - 1, Q, CH, CAP, B), i16),
            pltpu.VMEM((R - 1, 2, B), f32),
            pltpu.VMEM((R - 1, Q, 2, B), f32),
            pltpu.VMEM((L * 64, B), f32),
            pltpu.VMEM((L, NB * CH, B), i16),
            pltpu.VMEM((L, NB * CH, B), i16),
            pltpu.VMEM((L, 1, B), f32),
            pltpu.VMEM((L, 1, B), f32),
            pltpu.VMEM((T, NB * B), f32),
            pltpu.VMEM((T * 8, B), f32),
            dma((9,)),
            dma((L,)),
            dma((R - 1,)),
            dma(()),
            dma((2, L)),
            dma(()),
            dma(()),
            dma(()),
            dma(()),
            dma(()),
            dma(()),
            dma(()),
            dma(()),
            dma((2,)),
        ],
        compiler_params=pltpu.CompilerParams(
            collective_id=0, has_side_effects=True, vmem_limit_bytes=48 * 2**20
        ),
        name="window",
    )(
        *(
            pltpu.with_memory_space_constraint(a, pltpu.HBM)
            for a in (
                block_flags.T,
                trace,
                lr_source.reshape(R, CAP),
                lr_count.reshape(1, R),
                lr_target.reshape(R, CAP),
                g_decay.reshape(NB, B),
                v_decay.reshape(NB, B),
                g_start.reshape(NB, B),
                v_start.reshape(NB, B),
                w_region.reshape(L * NB * B, NB * B),
                lr_weight.reshape(R, CAP, B, B),
            )
        )
    )
    membrane, g_last = pl.pallas_call(
        place,
        out_shape=(
            jax.ShapeDtypeStruct((T, NB * B), f32),
            jax.ShapeDtypeStruct((NB, B), f32),
        ),
        in_specs=[vmem, vmem],
        out_specs=(hbm, hbm),
        scratch_shapes=[dma((2,))],
        compiler_params=pltpu.CompilerParams(vmem_limit_bytes=2**20),
        name="place",
    )(membrane, g_last)
    return membrane, g_last.reshape(NB * B)


def solution(mesh):
    return jax.shard_map(
        local,
        mesh=mesh,
        in_specs=(
            P(None, ("region", "local")),
            P(None, ("region", "local")),
            P("region", None, "local"),
            P("region", "local", None, None, None, None),
            P("region", "local", None, None),
            P("region", "local", None, None),
            P("region", "local", None),
            P(("region", "local")),
            P(("region", "local")),
            P(("region", "local")),
            P(("region", "local")),
        ),
        out_specs=(P(None, ("region", "local")), P(("region", "local"))),
        check_vma=False,
    )
```
